512 devices in a mesh: ka: 32 (over x, y, core), hist: 16 (over z).
Axes of the slice: x: 4, y: 4, z: 16, core: 2. Of those that a mesh axis runs over, the one named last changes fastest.
Arguments:
- green_row: float32 [1024, 576, 128], P('hist', 'ka'), may hold values from -6 to 6
- screened: float32 [1024, 576, 128], P('hist', 'ka'), may hold values from -0.2 to 0.2
- hamilton: float32 [576, 128], P('ka'), may hold values from -6 to 6
- equal_time: float32 [576, 128], P('ka'), may hold values from -0.5 to 2.5, as said below
- quad_class: int32 [1024], P('hist'), may hold values from 0 to 3
- live_count: int32 [16], P('hist'), may hold values from 1 to 64
Outputs:
- green_next: float32 [1024, 576, 128], P('hist', 'ka')
The draws below stay inside these ranges and needn't reach their ends.
Inputs may be any that keep to these rules, and one draw needn't show every extreme that they name: `quad_class`: class c selects the weight q[c] of q = (0.375, 1.1666666, 0.9583333, 1.0). Stored times at positions live_count[j] or later inside block j carry no weight. `equal_time`: the imaginary diagonal entries are positive.
All inputs are finite; a program needn't handle non-finite values.
Results may differ from the reference program's by a relative error of at most 0.00005.
Values sent between devices are 32-bit elements; how exact they have to be, the bound alone decides.
A program may use at most 64 MiB of HBM per device.

```python
import math
import jax
import jax.numpy as jnp
from jax import lax

SIDE = 24
BANDS = 8
TB = 64
NT = 1024
NK = 576
N_HIST = 16


def draw_equal_time(key, part):
    points = SIDE * SIDE
    width = 2 * BANDS * BANDS
    first_key = jax.random.fold_in(key, 11)
    second_key = jax.random.fold_in(key, 23)
    base = jnp.clip(0.1 * jax.random.normal(first_key, (points, width), jnp.float32), -0.5, 0.5)
    ramp = 1.0 + 2.0 * jnp.arange(points, dtype=jnp.float32) / (points - 1)
    occupied = jax.random.uniform(second_key, (points, BANDS), jnp.float32, 0.1, 0.6)
    occupied = occupied * ramp[:, None]
    spots = BANDS * BANDS + jnp.arange(BANDS, dtype=jnp.int32) * (BANDS + 1)
    placing = (jnp.arange(width, dtype=jnp.int32)[None, :] == spots[:, None]).astype(jnp.float32)
    return base * (1.0 - jnp.sum(placing, axis=0))[None, :] + jnp.dot(occupied, placing)


def with_ends(result, stream_key, least, high):
    dims = result.shape
    spot = [jax.random.randint(jax.random.fold_in(stream_key, axis), (), 0, dims[axis]) for axis in range(len(dims))]
    result = result.at[tuple(spot)].set(least)
    longest = dims.index(max(dims))
    spot[longest] = (spot[longest] + 1) % dims[longest]
    return result.at[tuple(spot)].set(high)


def shard_levels(rng, extent, cuts, least, largest):
    factor_of, own = 1.0, jax.random.fold_in(rng, 6)
    for dim, parts in cuts:
        steps = jnp.exp(jax.random.uniform(jax.random.fold_in(own, dim), (parts,), jnp.float32, least / len(cuts), largest / len(cuts)))
        factor_of = factor_of * jnp.repeat(steps, extent[dim] // parts).reshape([-1 if axis == dim else 1 for axis in range(len(extent))])
    return factor_of


def gaussian(rng, shape, deviation, most, shards=(), kind=jnp.bfloat16):
    drawn = deviation * jax.random.normal(rng, shape, jnp.float32)
    if shards:
        drawn = drawn * shard_levels(rng, shape, shards, -0.22, 0.18)
    return jnp.clip(drawn, -most, most).astype(kind)


def setup_inputs(seed: int = 0) -> dict:
    splits = jax.random.split(jax.random.key(seed), 7)
    green_row = gaussian(splits[0], (NT, NK, 2 * BANDS * BANDS), 1.0, 6.0, ((0, 16), (1, 32)), jnp.float32)
    screened = gaussian(splits[1], (NT, NK, 2 * BANDS * BANDS), 0.03, 0.2, ((0, 16), (1, 32)), jnp.float32)
    hamilton = gaussian(splits[2], (NK, 2 * BANDS * BANDS), 1.0, 6.0, ((0, 32),), jnp.float32)
    equal_time = draw_equal_time(jax.random.fold_in(splits[6], 71), 0)
    quad_class = with_ends(jax.random.randint(splits[4], (NT,), 0, 4), jax.random.fold_in(splits[4], 1), 0, 3).astype(jnp.int32)
    live_count = with_ends(jax.random.randint(splits[5], (N_HIST,), 1, TB + 1), jax.random.fold_in(splits[5], 1), 1, TB).astype(jnp.int32)
    return {"green_row": green_row, "screened": screened, "hamilton": hamilton, "equal_time": equal_time, "quad_class": quad_class, "live_count": live_count}


time_step = 0.1
hubbard = 1.0
quadrature = (0.375, 1.1666666, 0.9583333, 1.0)


def phase_tables(side):
    points = jnp.arange(side * side, dtype=jnp.int32)
    first_axis = points // side
    second = points % side
    winding = (first_axis[:, None] * first_axis[None, :] + second[:, None] * second[None, :]) % side
    angles = winding.astype(jnp.float32) * (2.0 * math.pi / side)
    return jnp.cos(angles) / side, jnp.sin(angles) / side


def transform(phases, values):
    return jnp.einsum("rk,tke->tre", phases, values, precision=lax.Precision.HIGHEST)


def self_energy(greens, screen, cosine_table, sine_table):
    entries = greens.shape[-1] // 2
    green_real, green_imag = greens[..., :entries], greens[..., entries:]
    lattice_real = transform(cosine_table, green_real) + transform(sine_table, green_imag)
    lattice_imag = transform(cosine_table, green_imag) - transform(sine_table, green_real)
    screen_real, screen_imag = screen[..., :entries], screen[..., entries:]
    sigma_real = -(lattice_real * screen_imag + lattice_imag * screen_real)
    sigma_imag = lattice_real * screen_real - lattice_imag * screen_imag
    back_real = transform(cosine_table, sigma_real) - transform(sine_table, sigma_imag)
    back_imag = transform(cosine_table, sigma_imag) + transform(sine_table, sigma_real)
    return back_real, back_imag


def contract(self_real, self_imag, greens, weights):
    history, points, width = greens.shape
    entries = width // 2
    matrix_shape = (history, points, BANDS, BANDS)
    weighted_real = (self_real * weights[:, None, None]).reshape(matrix_shape)
    weighted_imag = (self_imag * weights[:, None, None]).reshape(matrix_shape)
    green_real = greens[..., :entries].reshape(matrix_shape)
    green_imag = greens[..., entries:].reshape(matrix_shape)
    highest = lax.Precision.HIGHEST
    out_real = -(jnp.einsum("tkab,tkcb->kac", weighted_real, green_real, precision=highest)
                 + jnp.einsum("tkab,tkcb->kac", weighted_imag, green_imag, precision=highest))
    out_imag = (jnp.einsum("tkab,tkcb->kac", weighted_real, green_imag, precision=highest)
                - jnp.einsum("tkab,tkcb->kac", weighted_imag, green_real, precision=highest))
    return jnp.concatenate([out_real.reshape(points, entries), out_imag.reshape(points, entries)], axis=1)


def propagate(greens, effective):
    history, points, width = greens.shape
    entries = width // 2
    matrix_shape = (history, points, BANDS, BANDS)
    green_real = greens[..., :entries].reshape(matrix_shape)
    green_imag = greens[..., entries:].reshape(matrix_shape)
    hamil_real = effective[:, :entries].reshape(points, BANDS, BANDS)
    hamil_imag = effective[:, entries:].reshape(points, BANDS, BANDS)
    highest = lax.Precision.HIGHEST
    prod_real = (jnp.einsum("kab,tkbc->tkac", hamil_real, green_real, precision=highest)
                 - jnp.einsum("kab,tkbc->tkac", hamil_imag, green_imag, precision=highest))
    prod_imag = (jnp.einsum("kab,tkbc->tkac", hamil_real, green_imag, precision=highest)
                 + jnp.einsum("kab,tkbc->tkac", hamil_imag, green_real, precision=highest))
    new_real = greens[..., :entries] + time_step * prod_imag.reshape(history, points, entries)
    new_imag = greens[..., entries:] - time_step * prod_real.reshape(history, points, entries)
    return jnp.concatenate([new_real, new_imag], axis=2)


def class_weights(quad_class):
    table = jnp.array(quadrature, jnp.float32)
    match = quad_class[:, None] == jnp.arange(4, dtype=jnp.int32)[None, :]
    return jnp.sum(jnp.where(match, table[None, :], jnp.float32(0.0)), axis=1)


def diagonal_mask(offset):
    width = 2 * BANDS * BANDS
    spots = offset + jnp.arange(BANDS, dtype=jnp.int32) * (BANDS + 1)
    return jnp.any(jnp.arange(width, dtype=jnp.int32)[:, None] == spots[None, :], axis=1).astype(jnp.float32)


def reference(green_row, screened, hamilton, equal_time, quad_class, live_count):
    points = SIDE * SIDE
    width = 2 * BANDS * BANDS
    cosine_table, sine_table = phase_tables(SIDE)
    position = jnp.arange(NT, dtype=jnp.int32)
    limits = live_count[position // TB]
    weights = jnp.where(position % TB < limits, time_step * class_weights(quad_class), jnp.float32(0.0))

    def collide(pieces):
        greens, screen, weight = pieces
        self_real, self_imag = self_energy(greens, screen, cosine_table, sine_table)
        return contract(self_real, self_imag, greens, weight)

    blocks = (green_row.reshape(N_HIST, TB, points, width), screened.reshape(N_HIST, TB, points, width),
              weights.reshape(N_HIST, TB))
    collision = jnp.sum(lax.map(collide, blocks), axis=0)
    density = jnp.sum(equal_time * diagonal_mask(BANDS * BANDS)[None, :]) / points
    effective = hamilton + collision + hubbard * density * diagonal_mask(0)[None, :]

    def advance(greens):
        return propagate(greens, effective)

    stepped = lax.map(advance, green_row.reshape(N_HIST, TB, points, width))
    return stepped.reshape(NT, points, width)
```

```python
import functools
import math

import jax
import jax.numpy as jnp
import numpy as np
from jax import lax
from jax.experimental import pallas as pl
from jax.experimental.pallas import tpu as pltpu
from jax.sharding import PartitionSpec as P

SIDE = 24
NK = SIDE * SIDE
TIME_STEP = 0.1
HUBBARD = 1.0
QUADRATURE = (0.375, 1.1666666, 0.9583333, 1.0)
MESH = pl.DeviceIdType.MESH
KA, HIST = 32, 16
NB = NK // KA
BLK = NK // 4

OFFSETS = sorted(
    ((dx, dy, dc) for dx in range(4) for dy in range(4) for dc in range(2) if dx or dy or dc),
    key=lambda p: -(min(p[0], 4 - p[0]) + min(p[1], 4 - p[1])),
)


def phase_tables():
    k = np.arange(NK)
    out = np.zeros((4, SIDE, 2 * NK), np.float64)
    for r in range(SIDE):
        t1 = 2 * math.pi * ((r * (k // SIDE)) % SIDE) / SIDE
        t2 = 2 * math.pi * ((r * (k % SIDE)) % SIDE) / SIDE
        c1, s1, c2, s2 = np.cos(t1), np.sin(t1), np.cos(t2), np.sin(t2)
        out[0, r] = np.concatenate([c1, s1]) / SIDE
        out[1, r] = np.concatenate([s1, -c1]) / SIDE
        out[2, r] = np.concatenate([c2, c2])
        out[3, r] = np.concatenate([s2, s2])
    return out.astype(np.float32)


def contract_table():
    out = np.zeros((16 * 128, 128), np.float32)
    for d in range(16):
        for i in range(128):
            p, a = i // 64, (i // 8) % 8
            block = (i // 8 + d) % 16
            q, c = block // 8, block % 8
            if p == q:
                out[d * 128 + i, 8 * a + c] = -1.0
            else:
                out[d * 128 + i, 64 + 8 * a + c] = 1.0 if p == 0 else -1.0
    return out


def spread_table():
    out = np.zeros((128, 16 * 128), np.float32)
    for p in range(2):
        for b in range(8):
            for q in range(2):
                for a in range(8):
                    for c in range(8):
                        col = (p * 8 + b) * 128 + q * 64 + a * 8 + c
                        if p == q:
                            out[64 + a * 8 + b, col] = 1.0
                        else:
                            out[a * 8 + b, col] = 1.0 if q == 0 else -1.0
    return out


def split(v):
    high = v.astype(jnp.bfloat16)
    return high, (v - high.astype(jnp.float32)).astype(jnp.bfloat16)


def dot(a, b):
    return jnp.dot(a, b, preferred_element_type=jnp.float32)


def dot3(ah, al, bh, bl):
    return dot(ah, bh) + (dot(al, bh) + dot(ah, bl))


def collide_kernel(
    g, w, ham, eq, qc, lc, tab, con, out,
    rg, rw, tabv, conv, mh, ml, yh, yl, lat, sig, gr, pr, part, tsum, hbuf,
    send, recv, lsem,
):
    me = lax.axis_index("ka")
    z = lax.axis_index("hist")
    x, y, c = me // 8, (me // 2) % 4, me % 2

    def peer(dx, dy, dc):
        return (lax.rem(x + dx, 4) * 4 + lax.rem(y + dy, 4)) * 2 + lax.rem(c + dc, 2)

    tab_copy = pltpu.make_async_copy(tab, tabv, lsem.at[0])
    con_copy = pltpu.make_async_copy(con, conv, lsem.at[1])
    barrier = pltpu.get_barrier_semaphore()
    for d in OFFSETS:
        pl.semaphore_signal(barrier, inc=1, device_id={"ka": peer(*d)}, device_id_type=MESH)
    for d in range(1, HIST):
        pl.semaphore_signal(barrier, inc=1, device_id={"hist": lax.rem(z + d, HIST)}, device_id_type=MESH)
    tab_copy.start()
    con_copy.start()
    pl.semaphore_wait(barrier, KA - 1 + HIST - 1)

    for n, (src, dst) in enumerate(((g, rg), (w, rw))):
        for d in OFFSETS:
            to = peer(*d)
            pltpu.make_async_remote_copy(
                src_ref=src.at[:, to], dst_ref=dst.at[me], send_sem=send.at[n], recv_sem=recv.at[n],
                device_id={"ka": to}, device_id_type=MESH,
            ).start()
        pltpu.make_async_copy(src.at[:, me], dst.at[me], recv.at[n]).start()

    def arrived(n, dst):
        pltpu.make_async_copy(dst, dst, recv.at[n]).wait()

    lane = lax.broadcasted_iota(jnp.int32, (8, 128), 1)
    sign = jnp.where(lane < 64, jnp.float32(1.0), jnp.float32(-1.0))

    tab_copy.wait()

    def build(i, _):
        rows = []
        for h in range(2):
            r1 = 2 * i + h
            a1, b1 = tabv[0, pl.ds(r1, 1), :], tabv[1, pl.ds(r1, 1), :]
            rows.append(a1 * tabv[2] - b1 * tabv[3])
        high, low = split(jnp.concatenate(rows, axis=0))
        at = pl.ds(pl.multiple_of(48 * i, 16), 48)
        mh[at, :] = high
        ml[at, :] = low
        return 0

    lax.fori_loop(0, SIDE // 2, build, 0)

    def weight(t):
        s = 2 * me + t
        q = qc[s]
        value = jnp.float32(0.0)
        for i in range(4):
            value = jnp.where(q == i, jnp.float32(np.float32(TIME_STEP) * np.float32(QUADRATURE[i])), value)
        return jnp.where(s < lc[0], value, jnp.float32(0.0))

    weights = (weight(0), weight(1))
    sign16 = jnp.concatenate([sign, sign], axis=0)
    rg2, rw2 = rg.reshape(2 * NK, 128), rw.reshape(2 * NK, 128)

    arrived(0, rg)

    def stage(i, _):
        at = pl.ds(pl.multiple_of(16 * i, 16), 16)
        at2 = pl.ds(pl.multiple_of(16 * i, 16) + NK, 16)
        for t in range(2):
            v = rg2[pl.ds(32 * i + t, 16, stride=2), :]
            turned = pltpu.roll(v, 64, 1) * sign16
            col = pl.ds(128 * t, 128)
            yh[at, col], yl[at, col] = split(v)
            yh[at2, col], yl[at2, col] = split(turned)
        return 0

    lax.fori_loop(0, NK // 16, stage, 0)

    def forward(i, _):
        at = pl.ds(pl.multiple_of(BLK * i, 16), BLK)
        lat[at, :] = dot3(mh[at, :], ml[at, :], yh[...], yl[...])
        return 0

    lax.fori_loop(0, 4, forward, 0)

    def rolled(i, _):
        at = pl.ds(pl.multiple_of(8 * i, 8), 8)
        for t in range(2):
            v = rg2[pl.ds(16 * i + t, 8, stride=2), :] * weights[t]
            for d in range(16):
                gr[t, d, at, :] = pltpu.roll(v, 128 - 8 * d, 1) if d else v
        return 0

    lax.fori_loop(0, NK // 8, rolled, 0)
    con_copy.wait()
    diag = (lax.broadcasted_iota(jnp.int32, (NB, 128), 1) - 64) % 9 == 0
    diag = diag & (lax.broadcasted_iota(jnp.int32, (NB, 128), 1) >= 64)
    occupied = jnp.sum(jnp.where(diag, eq[...], jnp.float32(0.0)))
    lane1 = lax.broadcasted_iota(jnp.int32, (1, 128), 1)
    density = jnp.where((lane1 % 9 == 0) & (lane1 < 64), occupied * jnp.float32(HUBBARD / NK / HIST), jnp.float32(0.0))

    arrived(1, rw)

    def product(i, _):
        at = pl.ds(pl.multiple_of(16 * i, 16), 16)
        at2 = pl.ds(pl.multiple_of(16 * i, 16) + NK, 16)
        real = sign16 > 0
        for t in range(2):
            col = pl.ds(128 * t, 128)
            v = rw2[pl.ds(32 * i + t, 16, stride=2), :]
            l = lat[at, col]
            same = l * v
            cross = l * pltpu.roll(v, 64, 1)
            s = jnp.where(real, -cross, -same) + pltpu.roll(jnp.where(real, same, -cross), 64, 1)
            turned = pltpu.roll(s, 64, 1) * (-sign16)
            yh[at, col], yl[at, col] = split(s)
            yh[at2, col], yl[at2, col] = split(turned)
        return 0

    lax.fori_loop(0, NK // 16, product, 0)

    def back(n, _):
        blk = lax.rem(x + 3 - n, 4)
        base = pl.multiple_of(BLK * blk, 16)
        at = pl.ds(base, BLK)
        sig[...] = dot3(mh[at, :], ml[at, :], yh[...], yl[...])

        def multiply(i, _):
            rows = pl.ds(pl.multiple_of(16 * i, 16), 16)
            grow = pl.ds(pl.multiple_of(base + 16 * i, 16), 16)
            s0, s1 = sig[rows, 0:128], sig[rows, 128:256]
            for d in range(16):
                v = s0 * gr[0, d, grow, :] + s1 * gr[1, d, grow, :]
                pr[0, rows, pl.ds(128 * d, 128)], pr[1, rows, pl.ds(128 * d, 128)] = split(v)
            return 0

        lax.fori_loop(0, BLK // 16, multiply, 0)
        part[at, :] = (dot(pr[0], conv[...]) + dot(pr[1], conv[...])) + density
        for d in range(8):
            to = blk * 8 + lax.rem(2 * y + c + 7 - d, 8)

            @pl.when(to != me)
            def _():
                pltpu.make_async_remote_copy(
                    src_ref=part.at[pl.ds(NB * to, NB)], dst_ref=tsum.at[me], send_sem=send.at[2], recv_sem=recv.at[2],
                    device_id={"ka": to}, device_id_type=MESH,
                ).start()

            @pl.when(to == me)
            def _():
                pltpu.make_async_copy(part.at[pl.ds(NB * to, NB)], tsum.at[me], recv.at[2]).start()
        return 0

    lax.fori_loop(0, 4, back, 0)
    arrived(2, tsum)
    hbuf[z] = jnp.sum(tsum[...], axis=0)
    for d in (8, 7, 9, 6, 10, 5, 11, 4, 12, 3, 13, 2, 14, 1, 15):
        pltpu.make_async_remote_copy(
            src_ref=hbuf.at[z], dst_ref=hbuf.at[z], send_sem=send.at[3], recv_sem=recv.at[3],
            device_id={"hist": lax.rem(z + d, HIST)}, device_id_type=MESH,
        ).start()
    some = hbuf.at[pl.ds(0, HIST - 1)]
    pltpu.make_async_copy(some, some, recv.at[3]).wait()
    out[...] = ham[...] + jnp.sum(hbuf[...], axis=0)

    for n, ref in enumerate((rg, rw)):
        sent = ref.at[pl.ds(0, KA - 1)]
        pltpu.make_async_copy(sent, sent, send.at[n]).wait()
    sent = tsum.at[pl.ds(0, KA - 1)]
    pltpu.make_async_copy(sent, sent, send.at[2]).wait()
    pltpu.make_async_copy(some, some, send.at[3]).wait()


def propagate_kernel(eff, g, spread, out, coef):
    step = pl.program_id(0)
    per = g.shape[0]

    @pl.when(step == 0)
    def _():
        e = eff[...]
        high, rest = split(e)
        mid = (e - high.astype(jnp.float32)) - rest.astype(jnp.float32)
        low = mid.astype(jnp.bfloat16)
        full = dot(high, spread[...]) + (dot(rest, spread[...]) + dot(low, spread[...]))
        full = full * jnp.float32(TIME_STEP)
        for pb in range(16):
            coef[pb] = full[:, 128 * pb : 128 * (pb + 1)]

    lane = lax.broadcasted_iota(jnp.int32, (8, 128), 1)
    keep = lane % 8 == lax.broadcasted_iota(jnp.int32, (8, 128), 0)
    for j in range(per):
        k = step * per + j
        rows = [
            jnp.where(keep, jnp.broadcast_to(coef[pb, pl.ds(k, 1), :], (8, 128)), jnp.float32(0.0)) for pb in range(16)
        ]
        mh, ml = split(jnp.concatenate(rows, axis=0))
        v = g[j]
        vh, vl = split(v)
        out[j] = v + dot3(vh, vl, mh, ml)


def per_device(green_row, screened, hamilton, equal_time, quad_class, live_count):
    nb, tb = NB, green_row.shape[0]
    g3 = green_row.transpose(1, 0, 2)
    w3 = screened.transpose(1, 0, 2)
    f32, bf16 = jnp.float32, jnp.bfloat16
    vmem, anywhere, smem = (pl.BlockSpec(memory_space=s) for s in (pltpu.VMEM, pl.ANY, pltpu.SMEM))
    eff = pl.pallas_call(
        collide_kernel,
        out_shape=jax.ShapeDtypeStruct((nb, 128), f32),
        in_specs=[anywhere, anywhere, vmem, vmem, smem, smem, anywhere, anywhere],
        out_specs=vmem,
        scratch_shapes=[
            pltpu.VMEM((KA, nb, 2, 128), f32),
            pltpu.VMEM((KA, nb, 2, 128), f32),
            pltpu.VMEM((4, SIDE, 2 * NK), f32),
            pltpu.VMEM((2048, 128), bf16),
            pltpu.VMEM((NK, 2 * NK), bf16),
            pltpu.VMEM((NK, 2 * NK), bf16),
            pltpu.VMEM((2 * NK, 256), bf16),
            pltpu.VMEM((2 * NK, 256), bf16),
            pltpu.VMEM((NK, 256), f32),
            pltpu.VMEM((BLK, 256), f32),
            pltpu.VMEM((2, 16, NK, 128), f32),
            pltpu.VMEM((2, BLK, 2048), bf16),
            pltpu.VMEM((NK, 128), f32),
            pltpu.VMEM((KA, nb, 128), f32),
            pltpu.VMEM((HIST, nb, 128), f32),
            pltpu.SemaphoreType.DMA((4,)),
            pltpu.SemaphoreType.DMA((4,)),
            pltpu.SemaphoreType.DMA((2,)),
        ],
        compiler_params=pltpu.CompilerParams(collective_id=0, has_side_effects=True, vmem_limit_bytes=48 << 20),
        name="collide",
    )(
        g3.reshape(nb, KA, 2, 128), w3.reshape(nb, KA, 2, 128), hamilton, equal_time, quad_class, live_count,
        jnp.asarray(phase_tables()), jnp.asarray(contract_table(), dtype=bf16),
    )
    per = 3
    stepped = pl.pallas_call(
        propagate_kernel,
        out_shape=jax.ShapeDtypeStruct((nb, tb, 128), f32),
        grid=(nb // per,),
        in_specs=[
            pl.BlockSpec((nb, 128), lambda i: (0, 0)),
            pl.BlockSpec((per, tb, 128), lambda i: (i, 0, 0)),
            pl.BlockSpec((128, 2048), lambda i: (0, 0)),
        ],
        out_specs=pl.BlockSpec((per, tb, 128), lambda i: (i, 0, 0)),
        scratch_shapes=[pltpu.VMEM((16, nb, 128), f32)],
        name="propagate",
    )(eff, g3, jnp.asarray(spread_table(), dtype=bf16))
    return stepped.transpose(1, 0, 2)


def solution(mesh):
    in_specs = (
        P("hist", "ka", None), P("hist", "ka", None), P("ka", None), P("ka", None), P("hist"), P("hist"),
    )
    return jax.shard_map(
        per_device, mesh=mesh, in_specs=in_specs, out_specs=P("hist", "ka", None), check_vma=False
    )
```

```python
import functools
import math

import jax
import jax.numpy as jnp
import numpy as np
from jax import lax
from jax.experimental import pallas as pl
from jax.experimental.pallas import tpu as pltpu
from jax.sharding import PartitionSpec as P

SIDE = 24
NK = SIDE * SIDE
TIME_STEP = 0.1
HUBBARD = 1.0
QUADRATURE = (0.375, 1.1666666, 0.9583333, 1.0)
MESH = pl.DeviceIdType.MESH
KA, HIST = 32, 16
NB = NK // KA
BLK = NK // 4

OFFSETS = sorted(
    ((dx, dy, dc) for dx in range(4) for dy in range(4) for dc in range(2) if dx or dy or dc),
    key=lambda p: -(min(p[0], 4 - p[0]) + min(p[1], 4 - p[1])),
)


def phase_tables():
    k = np.arange(NK)
    out = np.zeros((4, SIDE, 2 * NK), np.float64)
    for r in range(SIDE):
        t1 = 2 * math.pi * ((r * (k // SIDE)) % SIDE) / SIDE
        t2 = 2 * math.pi * ((r * (k % SIDE)) % SIDE) / SIDE
        c1, s1, c2, s2 = np.cos(t1), np.sin(t1), np.cos(t2), np.sin(t2)
        out[0, r] = np.concatenate([c1, s1]) / SIDE
        out[1, r] = np.concatenate([s1, -c1]) / SIDE
        out[2, r] = np.concatenate([c2, c2])
        out[3, r] = np.concatenate([s2, s2])
    return out.astype(np.float32)


def contract_table():
    out = np.zeros((16 * 128, 128), np.float32)
    for d in range(16):
        for i in range(128):
            p, a = i // 64, (i // 8) % 8
            block = (i // 8 + d) % 16
            q, c = block // 8, block % 8
            if p == q:
                out[d * 128 + i, 8 * a + c] = -1.0
            else:
                out[d * 128 + i, 64 + 8 * a + c] = 1.0 if p == 0 else -1.0
    return out


def split(v):
    high = v.astype(jnp.bfloat16)
    return high, (v - high.astype(jnp.float32)).astype(jnp.bfloat16)


def dot(a, b):
    return jnp.dot(a, b, preferred_element_type=jnp.float32)


def dot3(ah, al, bh, bl):
    return dot(ah, bh) + (dot(al, bh) + dot(ah, bl))


def collide_kernel(
    g, w, ham_in, eq_in, qc_in, lc, tab, con, out,
    ham, eq, qc, rg, rw, tabv, conv, mh, ml, yh, yl, lat, sig, gr, pr, part, tsum, hbuf,
    send, recv, lsem, go,
):
    me = lax.axis_index("ka")
    z = lax.axis_index("hist")
    x, y, c = me // 8, (me // 2) % 4, me % 2

    def peer(dx, dy, dc):
        return (lax.rem(x + dx, 4) * 4 + lax.rem(y + dy, 4)) * 2 + lax.rem(c + dc, 2)

    tab_copy = pltpu.make_async_copy(tab, tabv, lsem.at[0])
    con_copy = pltpu.make_async_copy(con, conv, lsem.at[1])
    small = [
        pltpu.make_async_copy(a, b, lsem.at[2 + i]) for i, (a, b) in enumerate(((qc_in, qc), (ham_in, ham), (eq_in, eq)))
    ]
    barrier = pltpu.get_barrier_semaphore()
    chip = me // 2
    for d in range(1, 16):
        pl.semaphore_signal(barrier, inc=1, device_id={"ka": 2 * lax.rem(chip + d, 16)}, device_id_type=MESH)

    @pl.when(c == 1)
    def _():
        pl.semaphore_signal(barrier, inc=1, device_id={"ka": me - 1}, device_id_type=MESH)

    tab_copy.start()
    con_copy.start()
    for copy in small:
        copy.start()

    @pl.when(c == 0)
    def _():
        pl.semaphore_wait(barrier, KA - 1)
        pl.semaphore_signal(go.at[0], inc=1, device_id={"ka": me + 1}, device_id_type=MESH)

    @pl.when(c == 1)
    def _():
        pl.semaphore_wait(go.at[0], 1)

    for n, (src, dst) in enumerate(((g, rg), (w, rw))):
        for d in OFFSETS:
            to = peer(*d)
            pltpu.make_async_remote_copy(
                src_ref=src.at[:, to], dst_ref=dst.at[me], send_sem=send.at[n], recv_sem=recv.at[n],
                device_id={"ka": to}, device_id_type=MESH,
            ).start()
        pltpu.make_async_copy(src.at[:, me], dst.at[me], recv.at[n]).start()

    @pl.when(c == 1)
    def _():
        for d in range(1, HIST):
            pl.semaphore_signal(barrier, inc=1, device_id={"hist": lax.rem(z + d, HIST)}, device_id_type=MESH)

    def arrived(n, dst):
        pltpu.make_async_copy(dst, dst, recv.at[n]).wait()

    lane = lax.broadcasted_iota(jnp.int32, (8, 128), 1)
    sign = jnp.where(lane < 64, jnp.float32(1.0), jnp.float32(-1.0))

    tab_copy.wait()

    def build(i, _):
        rows = []
        for h in range(2):
            r1 = 2 * i + h
            a1, b1 = tabv[0, pl.ds(r1, 1), :], tabv[1, pl.ds(r1, 1), :]
            rows.append(a1 * tabv[2] - b1 * tabv[3])
        high, low = split(jnp.concatenate(rows, axis=0))
        at = pl.ds(pl.multiple_of(48 * i, 16), 48)
        mh[at, :] = high
        ml[at, :] = low
        return 0

    lax.fori_loop(0, SIDE // 2, build, 0)

    for copy in small:
        copy.wait()

    def weight(t):
        s = 2 * me + t
        q = qc[s]
        value = jnp.float32(0.0)
        for i in range(4):
            value = jnp.where(q == i, jnp.float32(np.float32(TIME_STEP) * np.float32(QUADRATURE[i])), value)
        return jnp.where(s < lc[0], value, jnp.float32(0.0))

    weights = (weight(0), weight(1))
    sign16 = jnp.concatenate([sign, sign], axis=0)
    rg2, rw2 = rg.reshape(2 * NK, 128), rw.reshape(2 * NK, 128)

    arrived(0, rg)

    def stage(i, _):
        for u in range(3):
            row = pl.multiple_of(48 * i + 16 * u, 16)
            at, at2 = pl.ds(row, 16), pl.ds(row + NK, 16)
            for t in range(2):
                v = rg2[pl.ds(2 * row + t, 16, stride=2), :]
                turned = pltpu.roll(v, 64, 1) * sign16
                col = pl.ds(128 * t, 128)
                yh[at, col], yl[at, col] = split(v)
                yh[at2, col], yl[at2, col] = split(turned)
        return 0

    lax.fori_loop(0, NK // 48, stage, 0)

    def forward(i, _):
        at = pl.ds(pl.multiple_of(BLK * i, 16), BLK)
        v = dot3(mh[at, :], ml[at, :], yh[...], yl[...])
        lat[0, at, :] = v
        for t in range(2):
            lat[1, at, pl.ds(128 * t, 128)] = pltpu.roll(v[:, 128 * t : 128 * (t + 1)], 64, 1)
        return 0

    lax.fori_loop(0, 4, forward, 0)

    def rolled(i, _):
        for u in range(4):
            row = pl.multiple_of(32 * i + 8 * u, 8)
            for t in range(2):
                v = rg2[pl.ds(2 * row + t, 8, stride=2), :] * weights[t]
                for d in range(16):
                    gr[t, d, pl.ds(row, 8), :] = pltpu.roll(v, 128 - 8 * d, 1) if d else v
        return 0

    lax.fori_loop(0, NK // 32, rolled, 0)
    con_copy.wait()
    diag = (lax.broadcasted_iota(jnp.int32, (NB, 128), 1) - 64) % 9 == 0
    diag = diag & (lax.broadcasted_iota(jnp.int32, (NB, 128), 1) >= 64)
    occupied = jnp.sum(jnp.where(diag, eq[...], jnp.float32(0.0)))
    lane1 = lax.broadcasted_iota(jnp.int32, (1, 128), 1)
    density = jnp.where((lane1 % 9 == 0) & (lane1 < 64), occupied * jnp.float32(HUBBARD / NK / HIST), jnp.float32(0.0))

    arrived(1, rw)

    real = sign16 > 0

    def product(i, _):
        for u in range(3):
            row = pl.multiple_of(48 * i + 16 * u, 16)
            at, at2 = pl.ds(row, 16), pl.ds(row + NK, 16)
            for t in range(2):
                col = pl.ds(128 * t, 128)
                v = rw2[pl.ds(2 * row + t, 16, stride=2), :]
                same, cross = lat[0, at, col] * v, lat[1, at, col] * v
                own = -jnp.where(real, cross, same)
                other = jnp.where(real, same, -cross)
                s = own + pltpu.roll(other, 64, 1)
                turned = -sign16 * (pltpu.roll(own, 64, 1) + other)
                yh[at, col], yl[at, col] = split(s)
                yh[at2, col], yl[at2, col] = split(turned)
        return 0

    lax.fori_loop(0, NK // 48, product, 0)

    def back(n, _):
        blk = lax.rem(x + 3 - n, 4)
        base = pl.multiple_of(BLK * blk, 16)
        at = pl.ds(base, BLK)
        sig[...] = dot3(mh[at, :], ml[at, :], yh[...], yl[...])

        def multiply(i, _):
            for u in range(3):
                rows = pl.ds(pl.multiple_of(48 * i + 16 * u, 16), 16)
                grow = pl.ds(pl.multiple_of(base + 48 * i + 16 * u, 16), 16)
                s0, s1 = sig[rows, 0:128], sig[rows, 128:256]
                for d in range(16):
                    v = s0 * gr[0, d, grow, :] + s1 * gr[1, d, grow, :]
                    pr[0, rows, pl.ds(128 * d, 128)], pr[1, rows, pl.ds(128 * d, 128)] = split(v)
            return 0

        lax.fori_loop(0, BLK // 48, multiply, 0)
        part[at, :] = (dot(pr[0], conv[...]) + dot(pr[1], conv[...])) + density
        for d in range(8):
            to = blk * 8 + lax.rem(2 * y + c + 7 - d, 8)

            @pl.when(to != me)
            def _():
                pltpu.make_async_remote_copy(
                    src_ref=part.at[pl.ds(NB * to, NB)], dst_ref=tsum.at[me], send_sem=send.at[2], recv_sem=recv.at[2],
                    device_id={"ka": to}, device_id_type=MESH,
                ).start()

            @pl.when(to == me)
            def _():
                pltpu.make_async_copy(part.at[pl.ds(NB * to, NB)], tsum.at[me], recv.at[2]).start()
        return 0

    lax.fori_loop(0, 4, back, 0)

    @pl.when(c == 1)
    def _():
        pl.semaphore_wait(barrier, HIST - 1)
        pl.semaphore_signal(go.at[1], inc=1, device_id={"ka": me - 1}, device_id_type=MESH)

    arrived(2, tsum)
    hbuf[z] = jnp.sum(tsum[...], axis=0)

    @pl.when(c == 0)
    def _():
        pl.semaphore_wait(go.at[1], 1)

    for d in (8, 7, 9, 6, 10, 5, 11, 4, 12, 3, 13, 2, 14, 1, 15):
        pltpu.make_async_remote_copy(
            src_ref=hbuf.at[z], dst_ref=hbuf.at[z], send_sem=send.at[3], recv_sem=recv.at[3],
            device_id={"hist": lax.rem(z + d, HIST)}, device_id_type=MESH,
        ).start()
    some = hbuf.at[pl.ds(0, HIST - 1)]
    pltpu.make_async_copy(some, some, recv.at[3]).wait()
    out[pl.ds(0, NB), :] = ham[...] + jnp.sum(hbuf[...], axis=0)
    out[pl.ds(NB, 24 - NB), :] = jnp.zeros((24 - NB, 128), jnp.float32)

    for n, ref in enumerate((rg, rw)):
        sent = ref.at[pl.ds(0, KA - 1)]
        pltpu.make_async_copy(sent, sent, send.at[n]).wait()
    sent = tsum.at[pl.ds(0, KA - 1)]
    pltpu.make_async_copy(sent, sent, send.at[2]).wait()
    pltpu.make_async_copy(some, some, send.at[3]).wait()


def propagate_kernel(eff, g, out, gv, ov, coef, sem):
    nb = g.shape[0]
    groups = 3
    per = nb // groups
    fetch = [pltpu.make_async_copy(g.at[pl.ds(per * i, per)], gv.at[pl.ds(per * i, per)], sem.at[i]) for i in range(groups)]
    for copy in fetch:
        copy.start()

    e = eff[...] * jnp.float32(TIME_STEP)
    lane = lax.broadcasted_iota(jnp.int32, e.shape, 1)
    second = lane // 64
    for p in range(2):
        for b in range(8):
            from_imag = second == p
            index = jnp.where(from_imag, 64, 0) + (lane // 8) % 8 * 8 + b
            v = jnp.take_along_axis(e, index, axis=1)
            coef[8 * p + b] = jnp.where(from_imag | (second == 0), v, -v)

    lane8 = lax.broadcasted_iota(jnp.int32, (8, 128), 1)
    keep = lane8 % 8 == lax.broadcasted_iota(jnp.int32, (8, 128), 0)
    flush = []
    for i in range(groups):
        fetch[i].wait()
        for k in range(per * i, per * (i + 1)):
            rows = [
                jnp.where(keep, jnp.broadcast_to(coef[pb, pl.ds(k, 1), :], (8, 128)), jnp.float32(0.0)) for pb in range(16)
            ]
            mh, ml = split(jnp.concatenate(rows, axis=0))
            v = gv[k]
            vh, vl = split(v)
            ov[k] = v + dot3(vh, vl, mh, ml)
        copy = pltpu.make_async_copy(ov.at[pl.ds(per * i, per)], out.at[pl.ds(per * i, per)], sem.at[groups + i])
        copy.start()
        flush.append(copy)
    for copy in flush:
        copy.wait()


def per_device(green_row, screened, hamilton, equal_time, quad_class, live_count):
    nb, tb = NB, green_row.shape[0]
    g3 = green_row.transpose(1, 0, 2)
    w3 = screened.transpose(1, 0, 2)
    f32, bf16 = jnp.float32, jnp.bfloat16
    vmem, hbm, smem = (pl.BlockSpec(memory_space=s) for s in (pltpu.VMEM, pltpu.HBM, pltpu.SMEM))
    eff = pl.pallas_call(
        collide_kernel,
        out_shape=jax.ShapeDtypeStruct((24, 128), f32),
        in_specs=[hbm, hbm, hbm, hbm, hbm, smem, hbm, hbm],
        out_specs=vmem,
        scratch_shapes=[
            pltpu.VMEM((nb, 128), f32),
            pltpu.VMEM((nb, 128), f32),
            pltpu.SMEM((tb,), jnp.int32),
            pltpu.VMEM((KA, nb, 2, 128), f32),
            pltpu.VMEM((KA, nb, 2, 128), f32),
            pltpu.VMEM((4, SIDE, 2 * NK), f32),
            pltpu.VMEM((2048, 128), bf16),
            pltpu.VMEM((NK, 2 * NK), bf16),
            pltpu.VMEM((NK, 2 * NK), bf16),
            pltpu.VMEM((2 * NK, 256), bf16),
            pltpu.VMEM((2 * NK, 256), bf16),
            pltpu.VMEM((2, NK, 256), f32),
            pltpu.VMEM((BLK, 256), f32),
            pltpu.VMEM((2, 16, NK, 128), f32),
            pltpu.VMEM((2, BLK, 2048), bf16),
            pltpu.VMEM((NK, 128), f32),
            pltpu.VMEM((KA, nb, 128), f32),
            pltpu.VMEM((HIST, nb, 128), f32),
            pltpu.SemaphoreType.DMA((4,)),
            pltpu.SemaphoreType.DMA((4,)),
            pltpu.SemaphoreType.DMA((5,)),
            pltpu.SemaphoreType.REGULAR((2,)),
        ],
        compiler_params=pltpu.CompilerParams(collective_id=0, has_side_effects=True, vmem_limit_bytes=60 << 20),
        name="collide",
    )(
        g3.reshape(nb, KA, 2, 128), w3.reshape(nb, KA, 2, 128), hamilton, equal_time, quad_class, live_count,
        jnp.asarray(phase_tables()), jnp.asarray(contract_table(), dtype=bf16),
    )
    stepped = pl.pallas_call(
        propagate_kernel,
        out_shape=jax.ShapeDtypeStruct((nb, tb, 128), f32),
        in_specs=[vmem, hbm],
        out_specs=hbm,
        scratch_shapes=[
            pltpu.VMEM((nb, tb, 128), f32),
            pltpu.VMEM((nb, tb, 128), f32),
            pltpu.VMEM((16, 24, 128), f32),
            pltpu.SemaphoreType.DMA((6,)),
        ],
        name="propagate",
    )(eff, g3)
    return stepped.transpose(1, 0, 2)


def solution(mesh):
    in_specs = (
        P("hist", "ka", None), P("hist", "ka", None), P("ka", None), P("ka", None), P("hist"), P("hist"),
    )
    return jax.shard_map(
        per_device, mesh=mesh, in_specs=in_specs, out_specs=P("hist", "ka", None), check_vma=False
    )
```

```python
import functools
import math

import jax
import jax.numpy as jnp
import numpy as np
from jax import lax
from jax.experimental import pallas as pl
from jax.experimental.pallas import tpu as pltpu
from jax.sharding import PartitionSpec as P

SIDE = 24
NK = SIDE * SIDE
TIME_STEP = 0.1
HUBBARD = 1.0
QUADRATURE = (0.375, 1.1666666, 0.9583333, 1.0)
MESH = pl.DeviceIdType.MESH
KA, HIST = 32, 16
NB = NK // KA
BLK = NK // 4

OFFSETS = sorted(
    ((dx, dy, dc) for dx in range(4) for dy in range(4) for dc in range(2) if dx or dy or dc),
    key=lambda p: -(min(p[0], 4 - p[0]) + min(p[1], 4 - p[1])),
)


def phase_tables():
    col = np.arange(BLK)
    major, minor = col // SIDE, col % SIDE
    out = np.zeros((2, 4, SIDE, 2 * BLK), np.float64)
    for i in range(SIDE):
        m, part = i // 6, i % 6
        for way, turn in ((0, (4 * part + m) * major), (1, part * (4 * major + m))):
            t1 = 2 * math.pi * (turn % SIDE) / SIDE
            t2 = 2 * math.pi * ((i * minor) % SIDE) / SIDE
            c1, s1, c2, s2 = np.cos(t1), np.sin(t1), np.cos(t2), np.sin(t2)
            out[way, 0, i] = np.concatenate([c1, s1]) / SIDE
            out[way, 1, i] = np.concatenate([s1, -c1]) / SIDE
            out[way, 2, i] = np.concatenate([c2, c2])
            out[way, 3, i] = np.concatenate([s2, s2])
    return out.astype(np.float32)


def contract_table():
    out = np.zeros((16 * 128, 128), np.float32)
    for d in range(16):
        for i in range(128):
            p, a = i // 64, (i // 8) % 8
            block = (i // 8 + d) % 16
            q, c = block // 8, block % 8
            if p == q:
                out[d * 128 + i, 8 * a + c] = -1.0
            else:
                out[d * 128 + i, 64 + 8 * a + c] = 1.0 if p == 0 else -1.0
    return out


def split(v):
    high = v.astype(jnp.bfloat16)
    return high, (v - high.astype(jnp.float32)).astype(jnp.bfloat16)


def dot(a, b):
    return jnp.dot(a, b, preferred_element_type=jnp.float32)


def dot3(ah, al, bh, bl):
    return dot(ah, bh) + (dot(al, bh) + dot(ah, bl))


def collide_kernel(
    g, w, ham_in, eq_in, qc_in, lc, tab, con, out,
    ham, eq, qc, rg, rw, tabv, conv, mh, ml, yh, yl, lat, sig, gr, pr, part, tsum, hbuf,
    send, recv, lsem, go,
):
    me = lax.axis_index("ka")
    z = lax.axis_index("hist")
    x, y, c = me // 8, (me // 2) % 4, me % 2

    def peer(dx, dy, dc):
        return (lax.rem(x + dx, 4) * 4 + lax.rem(y + dy, 4)) * 2 + lax.rem(c + dc, 2)

    tab_copy = pltpu.make_async_copy(tab, tabv, lsem.at[0])
    con_copy = pltpu.make_async_copy(con, conv, lsem.at[1])
    small = [
        pltpu.make_async_copy(a, b, lsem.at[2 + i]) for i, (a, b) in enumerate(((qc_in, qc), (ham_in, ham), (eq_in, eq)))
    ]
    barrier = pltpu.get_barrier_semaphore()
    chip = me // 2
    for d in range(1, 16):
        pl.semaphore_signal(barrier, inc=1, device_id={"ka": 2 * lax.rem(chip + d, 16)}, device_id_type=MESH)

    @pl.when(c == 1)
    def _():
        pl.semaphore_signal(barrier, inc=1, device_id={"ka": me - 1}, device_id_type=MESH)

    tab_copy.start()
    con_copy.start()
    for copy in small:
        copy.start()

    @pl.when(c == 0)
    def _():
        pl.semaphore_wait(barrier, KA - 1)
        pl.semaphore_signal(go.at[0], inc=1, device_id={"ka": me + 1}, device_id_type=MESH)

    @pl.when(c == 1)
    def _():
        pl.semaphore_wait(go.at[0], 1)

    for n, (src, dst) in enumerate(((g, rg), (w, rw))):
        for d in OFFSETS:
            to = peer(*d)
            pltpu.make_async_remote_copy(
                src_ref=src.at[:, to], dst_ref=dst.at[me], send_sem=send.at[n], recv_sem=recv.at[n],
                device_id={"ka": to}, device_id_type=MESH,
            ).start()
        pltpu.make_async_copy(src.at[:, me], dst.at[me], recv.at[n]).start()

    @pl.when(c == 1)
    def _():
        for d in range(1, HIST):
            pl.semaphore_signal(barrier, inc=1, device_id={"hist": lax.rem(z + d, HIST)}, device_id_type=MESH)

    def arrived(n, dst):
        pltpu.make_async_copy(dst, dst, recv.at[n]).wait()

    lane = lax.broadcasted_iota(jnp.int32, (8, 128), 1)
    sign = jnp.where(lane < 64, jnp.float32(1.0), jnp.float32(-1.0))

    tab_copy.wait()

    def build(i, _):
        for way in range(2):
            rows = []
            for h in range(2):
                part = pl.ds(2 * i + h, 1)
                rows.append(tabv[way, 0, part, :] * tabv[way, 2] - tabv[way, 1, part, :] * tabv[way, 3])
            high, low = split(jnp.concatenate(rows, axis=0))
            at = pl.ds(pl.multiple_of(48 * i, 16), 48)
            mh[way, at, :] = high
            ml[way, at, :] = low
        return 0

    lax.fori_loop(0, SIDE // 2, build, 0)

    for copy in small:
        copy.wait()

    def weight(t):
        s = 2 * me + t
        q = qc[s]
        value = jnp.float32(0.0)
        for i in range(4):
            value = jnp.where(q == i, jnp.float32(np.float32(TIME_STEP) * np.float32(QUADRATURE[i])), value)
        return jnp.where(s < lc[0], value, jnp.float32(0.0))

    weights = (weight(0), weight(1))
    sign16 = jnp.concatenate([sign, sign], axis=0)
    rg2, rw2 = rg.reshape(2 * NK, 128), rw.reshape(2 * NK, 128)

    arrived(0, rg)

    def put(m, row, t, v, turned):
        col = pl.ds(128 * t, 128)
        yh[m, pl.ds(row, 16), col], yl[m, pl.ds(row, 16), col] = split(v)
        yh[m, pl.ds(row + BLK, 16), col], yl[m, pl.ds(row + BLK, 16), col] = split(turned)

    def stage(i, _):
        row = pl.multiple_of(16 * i, 16)
        for t in range(2):
            v = [rg2[pl.ds(2 * (row + BLK * j) + t, 16, stride=2), :] for j in range(4)]
            w_ = [pltpu.roll(e, 64, 1) * sign16 for e in v]
            even, odd, even_, odd_ = v[0] + v[2], v[1] + v[3], w_[0] + w_[2], w_[1] + w_[3]
            put(0, row, t, even + odd, even_ + odd_)
            put(2, row, t, even - odd, even_ - odd_)
            even, odd, even_, odd_ = v[0] - v[2], v[1] - v[3], w_[0] - w_[2], w_[1] - w_[3]
            put(1, row, t, even + odd_, even_ - odd)
            put(3, row, t, even - odd_, even_ + odd)
        return 0

    lax.fori_loop(0, BLK // 16, stage, 0)

    def transform(way, m):
        at = pl.ds(BLK * m, BLK)
        return dot3(mh[way, at, :], ml[way, at, :], yh[m], yl[m])

    for m in range(4):
        v = transform(0, m)
        at = pl.ds(BLK * m, BLK)
        lat[0, at, :] = v
        for t in range(2):
            lat[1, at, pl.ds(128 * t, 128)] = pltpu.roll(v[:, 128 * t : 128 * (t + 1)], 64, 1)

    def rolled(i, _):
        for u in range(2):
            row = pl.multiple_of(32 * i + 16 * u, 16)
            for t in range(2):
                v = rg2[pl.ds(2 * row + t, 16, stride=2), :] * weights[t]
                for d in range(16):
                    gr[2 * i + u, 2 * d + t] = pltpu.roll(v, 128 - 8 * d, 1) if d else v
        return 0

    lax.fori_loop(0, NK // 32, rolled, 0)
    con_copy.wait()
    diag = (lax.broadcasted_iota(jnp.int32, (NB, 128), 1) - 64) % 9 == 0
    diag = diag & (lax.broadcasted_iota(jnp.int32, (NB, 128), 1) >= 64)
    occupied = jnp.sum(jnp.where(diag, eq[...], jnp.float32(0.0)))
    lane1 = lax.broadcasted_iota(jnp.int32, (1, 128), 1)
    density = jnp.where((lane1 % 9 == 0) & (lane1 < 64), occupied * jnp.float32(HUBBARD / NK / HIST), jnp.float32(0.0))

    arrived(1, rw)

    real = sign16 > 0

    def product(i, _):
        m, pair = i // 3, i % 3
        for u in range(3):
            row = pl.multiple_of(48 * pair + 16 * u, 16)
            at = pl.ds(pl.multiple_of(BLK * m + 48 * pair + 16 * u, 16), 16)
            for t in range(2):
                col = pl.ds(128 * t, 128)
                halves = []
                for h in range(2):
                    e = 2 * u + h
                    start = ((8 * pair + 4 * (e // 3) + m) * SIDE + 8 * (e % 3)) * 2 + t
                    halves.append(rw2[pl.ds(start, 8, stride=2), :])
                v = jnp.concatenate(halves, axis=0)
                same, cross = lat[0, at, col] * v, lat[1, at, col] * v
                own = -jnp.where(real, cross, same)
                other = jnp.where(real, same, -cross)
                put(m, row, t, own + pltpu.roll(other, 64, 1), -sign16 * (pltpu.roll(own, 64, 1) + other))
        return 0

    lax.fori_loop(0, 12, product, 0)

    e = [transform(1, m) for m in range(4)]
    diff = e[1] - e[3]
    across = [pltpu.roll(diff[:, 128 * t : 128 * (t + 1)], 64, 1) for t in range(2)]
    turn = jnp.where(lax.broadcasted_iota(jnp.int32, (BLK, 128), 1) < 64, jnp.float32(-1.0), jnp.float32(1.0))
    diff = jnp.concatenate([turn * part_ for part_ in across], axis=1)
    sig[0] = (e[0] + e[2]) + (e[1] + e[3])
    sig[2] = (e[0] + e[2]) - (e[1] + e[3])
    sig[1] = (e[0] - e[2]) + diff
    sig[3] = (e[0] - e[2]) - diff

    def block(n):
        return lax.rem(x + 3 - n, 4)

    for n in range(4):
        for i in range(BLK // 16):
            rows = pl.ds(16 * i, 16)
            s0, s1 = sig[block(n), rows, 0:128], sig[block(n), rows, 128:256]
            group = (BLK // 16) * block(n) + i
            for d in range(16):
                v = s0 * gr[group, 2 * d] + s1 * gr[group, 2 * d + 1]
                pr[n % 2, 0, rows, pl.ds(128 * d, 128)], pr[n % 2, 1, rows, pl.ds(128 * d, 128)] = split(v)
        at = pl.ds(pl.multiple_of(BLK * block(n), 16), BLK)
        part[at, :] = (dot(pr[n % 2, 0], conv[...]) + dot(pr[n % 2, 1], conv[...])) + density
        for d in range(8 if n < 3 else 7):
            to = block(n) * 8 + lax.rem(2 * y + c + 4 + d if n < 3 else 2 * y + c + 1 + d, 8)
            pltpu.make_async_remote_copy(
                src_ref=part.at[pl.ds(NB * to, NB)], dst_ref=tsum.at[me], send_sem=send.at[2], recv_sem=recv.at[2],
                device_id={"ka": to}, device_id_type=MESH,
            ).start()
    pltpu.make_async_copy(part.at[pl.ds(NB * me, NB)], tsum.at[me], recv.at[2]).start()

    @pl.when(c == 1)
    def _():
        pl.semaphore_wait(barrier, HIST - 1)
        pl.semaphore_signal(go.at[1], inc=1, device_id={"ka": me - 1}, device_id_type=MESH)

    arrived(2, tsum)
    hbuf[z] = jnp.sum(tsum[...], axis=0)

    @pl.when(c == 0)
    def _():
        pl.semaphore_wait(go.at[1], 1)

    for d in (8, 7, 9, 6, 10, 5, 11, 4, 12, 3, 13, 2, 14, 1, 15):
        pltpu.make_async_remote_copy(
            src_ref=hbuf.at[z], dst_ref=hbuf.at[z], send_sem=send.at[3], recv_sem=recv.at[3],
            device_id={"hist": lax.rem(z + d, HIST)}, device_id_type=MESH,
        ).start()
    some = hbuf.at[pl.ds(0, HIST - 1)]
    pltpu.make_async_copy(some, some, recv.at[3]).wait()
    out[pl.ds(0, NB), :] = ham[...] + jnp.sum(hbuf[...], axis=0)
    out[pl.ds(NB, 24 - NB), :] = jnp.zeros((24 - NB, 128), jnp.float32)

    for n, ref in enumerate((rg, rw)):
        sent = ref.at[pl.ds(0, KA - 1)]
        pltpu.make_async_copy(sent, sent, send.at[n]).wait()
    sent = tsum.at[pl.ds(0, KA - 1)]
    pltpu.make_async_copy(sent, sent, send.at[2]).wait()
    pltpu.make_async_copy(some, some, send.at[3]).wait()


def propagate_kernel(eff, g, out, gv, ov, coef, sem):
    nb = g.shape[0]
    groups = 3
    per = nb // groups
    fetch = [pltpu.make_async_copy(g.at[pl.ds(per * i, per)], gv.at[pl.ds(per * i, per)], sem.at[i]) for i in range(groups)]
    for copy in fetch:
        copy.start()

    e = eff[...] * jnp.float32(TIME_STEP)
    lane = lax.broadcasted_iota(jnp.int32, e.shape, 1)
    second = lane // 64
    for p in range(2):
        for b in range(8):
            from_imag = second == p
            index = jnp.where(from_imag, 64, 0) + (lane // 8) % 8 * 8 + b
            v = jnp.take_along_axis(e, index, axis=1)
            coef[8 * p + b] = jnp.where(from_imag | (second == 0), v, -v)

    lane8 = lax.broadcasted_iota(jnp.int32, (8, 128), 1)
    keep = lane8 % 8 == lax.broadcasted_iota(jnp.int32, (8, 128), 0)
    flush = []
    for i in range(groups):
        fetch[i].wait()
        for k in range(per * i, per * (i + 1)):
            rows = [
                jnp.where(keep, jnp.broadcast_to(coef[pb, pl.ds(k, 1), :], (8, 128)), jnp.float32(0.0)) for pb in range(16)
            ]
            mh, ml = split(jnp.concatenate(rows, axis=0))
            v = gv[k]
            vh, vl = split(v)
            ov[k] = v + dot3(vh, vl, mh, ml)
        copy = pltpu.make_async_copy(ov.at[pl.ds(per * i, per)], out.at[pl.ds(per * i, per)], sem.at[groups + i])
        copy.start()
        flush.append(copy)
    for copy in flush:
        copy.wait()


def per_device(green_row, screened, hamilton, equal_time, quad_class, live_count):
    nb, tb = NB, green_row.shape[0]
    g3 = green_row.transpose(1, 0, 2)
    w3 = screened.transpose(1, 0, 2)
    f32, bf16 = jnp.float32, jnp.bfloat16
    vmem, hbm, smem = (pl.BlockSpec(memory_space=s) for s in (pltpu.VMEM, pltpu.HBM, pltpu.SMEM))
    eff = pl.pallas_call(
        collide_kernel,
        out_shape=jax.ShapeDtypeStruct((24, 128), f32),
        in_specs=[hbm, hbm, hbm, hbm, hbm, smem, hbm, hbm],
        out_specs=vmem,
        scratch_shapes=[
            pltpu.VMEM((nb, 128), f32),
            pltpu.VMEM((nb, 128), f32),
            pltpu.SMEM((tb,), jnp.int32),
            pltpu.VMEM((KA, nb, 2, 128), f32),
            pltpu.VMEM((KA, nb, 2, 128), f32),
            pltpu.VMEM((2, 4, SIDE, 2 * BLK), f32),
            pltpu.VMEM((2048, 128), bf16),
            pltpu.VMEM((2, NK, 2 * BLK), bf16),
            pltpu.VMEM((2, NK, 2 * BLK), bf16),
            pltpu.VMEM((4, 2 * BLK, 256), bf16),
            pltpu.VMEM((4, 2 * BLK, 256), bf16),
            pltpu.VMEM((2, NK, 256), f32),
            pltpu.VMEM((4, BLK, 256), f32),
            pltpu.VMEM((NK // 16, 32, 16, 128), f32),
            pltpu.VMEM((2, 2, BLK, 2048), bf16),
            pltpu.VMEM((NK, 128), f32),
            pltpu.VMEM((KA, nb, 128), f32),
            pltpu.VMEM((HIST, nb, 128), f32),
            pltpu.SemaphoreType.DMA((4,)),
            pltpu.SemaphoreType.DMA((4,)),
            pltpu.SemaphoreType.DMA((5,)),
            pltpu.SemaphoreType.REGULAR((2,)),
        ],
        compiler_params=pltpu.CompilerParams(collective_id=0, has_side_effects=True, vmem_limit_bytes=60 << 20),
        name="collide",
    )(
        g3.reshape(nb, KA, 2, 128), w3.reshape(nb, KA, 2, 128), hamilton, equal_time, quad_class, live_count,
        jnp.asarray(phase_tables()), jnp.asarray(contract_table(), dtype=bf16),
    )
    stepped = pl.pallas_call(
        propagate_kernel,
        out_shape=jax.ShapeDtypeStruct((nb, tb, 128), f32),
        in_specs=[vmem, hbm],
        out_specs=hbm,
        scratch_shapes=[
            pltpu.VMEM((nb, tb, 128), f32),
            pltpu.VMEM((nb, tb, 128), f32),
            pltpu.VMEM((16, 24, 128), f32),
            pltpu.SemaphoreType.DMA((6,)),
        ],
        name="propagate",
    )(eff, g3)
    return stepped.transpose(1, 0, 2)


def solution(mesh):
    in_specs = (
        P("hist", "ka", None), P("hist", "ka", None), P("ka", None), P("ka", None), P("hist"), P("hist"),
    )
    return jax.shard_map(
        per_device, mesh=mesh, in_specs=in_specs, out_specs=P("hist", "ka", None), check_vma=False
    )
```

```python
import functools
import math

import jax
import jax.numpy as jnp
import numpy as np
from jax import lax
from jax.experimental import pallas as pl
from jax.experimental.pallas import tpu as pltpu
from jax.sharding import PartitionSpec as P

SIDE = 24
NK = SIDE * SIDE
TIME_STEP = 0.1
HUBBARD = 1.0
QUADRATURE = (0.375, 1.1666666, 0.9583333, 1.0)
MESH = pl.DeviceIdType.MESH
KA, HIST = 32, 16
NB = NK // KA
BLK = NK // 4

OFFSETS = sorted(
    ((dx, dy, dc) for dx in range(4) for dy in range(4) for dc in range(2) if dx or dy or dc),
    key=lambda p: -(min(p[0], 4 - p[0]) + min(p[1], 4 - p[1])),
)


def phase_tables():
    col = np.arange(BLK)
    major, minor = col // SIDE, col % SIDE
    out = np.zeros((2, 4, SIDE, 2 * BLK), np.float64)
    for i in range(SIDE):
        m, part = i // 6, i % 6
        for way, turn in ((0, (4 * part + m) * major), (1, part * (4 * major + m))):
            t1 = 2 * math.pi * (turn % SIDE) / SIDE
            t2 = 2 * math.pi * ((i * minor) % SIDE) / SIDE
            c1, s1, c2, s2 = np.cos(t1), np.sin(t1), np.cos(t2), np.sin(t2)
            out[way, 0, i] = np.concatenate([c1, s1]) / SIDE
            out[way, 1, i] = np.concatenate([s1, -c1]) / SIDE
            out[way, 2, i] = np.concatenate([c2, c2])
            out[way, 3, i] = np.concatenate([s2, s2])
    return out.astype(np.float32)


def contract_table():
    out = np.zeros((16 * 128, 128), np.float32)
    for d in range(16):
        for i in range(128):
            p, a = i // 64, (i // 8) % 8
            block = (i // 8 + d) % 16
            q, c = block // 8, block % 8
            if p == q:
                out[d * 128 + i, 8 * a + c] = -1.0
            else:
                out[d * 128 + i, 64 + 8 * a + c] = 1.0 if p == 0 else -1.0
    return out


def split(v):
    high = v.astype(jnp.bfloat16)
    return high, (v - high.astype(jnp.float32)).astype(jnp.bfloat16)


def dot(a, b):
    return jnp.dot(a, b, preferred_element_type=jnp.float32)


def dot3(ah, al, bh, bl):
    return dot(ah, bh) + (dot(al, bh) + dot(ah, bl))


def collide_kernel(
    g, w, ham_in, eq_in, qc_in, lc_in, tab, con, out,
    ham, eq, qc, lc, rg, rw, tabv, conv, mh, ml, yh, yl, lat, sig, gr, pr, part, tsum, hbuf,
    send, recv, lsem, go,
):
    me = lax.axis_index("ka")
    z = lax.axis_index("hist")
    x, y, c = me // 8, (me // 2) % 4, me % 2

    def peer(dx, dy, dc):
        return (lax.rem(x + dx, 4) * 4 + lax.rem(y + dy, 4)) * 2 + lax.rem(c + dc, 2)

    tab_copy = pltpu.make_async_copy(tab, tabv, lsem.at[0])
    con_copy = pltpu.make_async_copy(con, conv, lsem.at[1])
    small = [
        pltpu.make_async_copy(a, b, lsem.at[2 + i]) for i, (a, b) in enumerate(((qc_in, qc), (lc_in, lc), (ham_in, ham), (eq_in, eq)))
    ]
    barrier = pltpu.get_barrier_semaphore()
    chip = me // 2
    for d in range(1, 16):
        pl.semaphore_signal(barrier, inc=1, device_id={"ka": 2 * lax.rem(chip + d, 16)}, device_id_type=MESH)

    @pl.when(c == 1)
    def _():
        pl.semaphore_signal(barrier, inc=1, device_id={"ka": me - 1}, device_id_type=MESH)

    tab_copy.start()
    con_copy.start()
    for copy in small:
        copy.start()

    @pl.when(c == 0)
    def _():
        pl.semaphore_wait(barrier, KA - 1)
        pl.semaphore_signal(go.at[0], inc=1, device_id={"ka": me + 1}, device_id_type=MESH)

    @pl.when(c == 1)
    def _():
        pl.semaphore_wait(go.at[0], 1)

    for n, (src, dst) in enumerate(((g, rg), (w, rw))):
        for d in OFFSETS:
            to = peer(*d)
            pltpu.make_async_remote_copy(
                src_ref=src.at[:, to], dst_ref=dst.at[me], send_sem=send.at[n], recv_sem=recv.at[n],
                device_id={"ka": to}, device_id_type=MESH,
            ).start()
        pltpu.make_async_copy(src.at[:, me], dst.at[me], recv.at[n]).start()

    @pl.when(c == 1)
    def _():
        for d in range(1, HIST):
            pl.semaphore_signal(barrier, inc=1, device_id={"hist": lax.rem(z + d, HIST)}, device_id_type=MESH)

    def arrived(n, dst):
        pltpu.make_async_copy(dst, dst, recv.at[n]).wait()

    lane = lax.broadcasted_iota(jnp.int32, (8, 128), 1)
    sign = jnp.where(lane < 64, jnp.float32(1.0), jnp.float32(-1.0))

    tab_copy.wait()

    def build(i, _):
        for way in range(2):
            rows = []
            for h in range(2):
                part = pl.ds(2 * i + h, 1)
                rows.append(tabv[way, 0, part, :] * tabv[way, 2] - tabv[way, 1, part, :] * tabv[way, 3])
            high, low = split(jnp.concatenate(rows, axis=0))
            at = pl.ds(pl.multiple_of(48 * i, 16), 48)
            mh[way, at, :] = high
            ml[way, at, :] = low
        return 0

    lax.fori_loop(0, SIDE // 2, build, 0)

    for copy in small:
        copy.wait()

    def weight(t):
        s = 2 * me + t
        q = qc[s]
        value = jnp.float32(0.0)
        for i in range(4):
            value = jnp.where(q == i, jnp.float32(np.float32(TIME_STEP) * np.float32(QUADRATURE[i])), value)
        return jnp.where(s < lc[0, 0], value, jnp.float32(0.0))

    weights = (weight(0), weight(1))
    sign16 = jnp.concatenate([sign, sign], axis=0)
    rg2, rw2 = rg.reshape(2 * NK, 128), rw.reshape(2 * NK, 128)

    arrived(0, rg)

    def put(m, row, t, v, turned):
        col = pl.ds(128 * t, 128)
        yh[m, pl.ds(row, 16), col], yl[m, pl.ds(row, 16), col] = split(v)
        yh[m, pl.ds(row + BLK, 16), col], yl[m, pl.ds(row + BLK, 16), col] = split(turned)

    def stage(i, _):
        row = pl.multiple_of(16 * i, 16)
        for t in range(2):
            v = [rg2[pl.ds(2 * (row + BLK * j) + t, 16, stride=2), :] for j in range(4)]
            w_ = [pltpu.roll(e, 64, 1) * sign16 for e in v]
            even, odd, even_, odd_ = v[0] + v[2], v[1] + v[3], w_[0] + w_[2], w_[1] + w_[3]
            put(0, row, t, even + odd, even_ + odd_)
            put(2, row, t, even - odd, even_ - odd_)
            even, odd, even_, odd_ = v[0] - v[2], v[1] - v[3], w_[0] - w_[2], w_[1] - w_[3]
            put(1, row, t, even + odd_, even_ - odd)
            put(3, row, t, even - odd_, even_ + odd)
        return 0

    lax.fori_loop(0, BLK // 16, stage, 0)

    def transform(way, m):
        at = pl.ds(BLK * m, BLK)
        return dot3(mh[way, at, :], ml[way, at, :], yh[m], yl[m])

    for m in range(4):
        v = transform(0, m)
        at = pl.ds(BLK * m, BLK)
        lat[0, at, :] = v
        for t in range(2):
            lat[1, at, pl.ds(128 * t, 128)] = pltpu.roll(v[:, 128 * t : 128 * (t + 1)], 64, 1)

    def rolled(i, _):
        for u in range(2):
            row = pl.multiple_of(32 * i + 16 * u, 16)
            for t in range(2):
                v = rg2[pl.ds(2 * row + t, 16, stride=2), :] * weights[t]
                for d in range(16):
                    gr[2 * i + u, 2 * d + t] = pltpu.roll(v, 128 - 8 * d, 1) if d else v
        return 0

    lax.fori_loop(0, NK // 32, rolled, 0)
    con_copy.wait()
    diag = (lax.broadcasted_iota(jnp.int32, (NB, 128), 1) - 64) % 9 == 0
    diag = diag & (lax.broadcasted_iota(jnp.int32, (NB, 128), 1) >= 64)
    occupied = jnp.sum(jnp.where(diag, eq[...], jnp.float32(0.0)))
    lane1 = lax.broadcasted_iota(jnp.int32, (1, 128), 1)
    density = jnp.where((lane1 % 9 == 0) & (lane1 < 64), occupied * jnp.float32(HUBBARD / NK / HIST), jnp.float32(0.0))

    arrived(1, rw)

    real = sign16 > 0

    def product(i, _):
        for pair in range(3):
            m = i
            for u in range(3):
                row = pl.multiple_of(48 * pair + 16 * u, 16)
                at = pl.ds(pl.multiple_of(BLK * m + 48 * pair + 16 * u, 16), 16)
                for t in range(2):
                    col = pl.ds(128 * t, 128)
                    halves = []
                    for h in range(2):
                        e = 2 * u + h
                        start = ((8 * pair + 4 * (e // 3) + m) * SIDE + 8 * (e % 3)) * 2 + t
                        halves.append(rw2[pl.ds(start, 8, stride=2), :])
                    v = jnp.concatenate(halves, axis=0)
                    same, cross = lat[0, at, col] * v, lat[1, at, col] * v
                    own = -jnp.where(real, cross, same)
                    other = jnp.where(real, same, -cross)
                    put(m, row, t, own + pltpu.roll(other, 64, 1), -sign16 * (pltpu.roll(own, 64, 1) + other))
        return 0

    lax.fori_loop(0, 4, product, 0)

    e = [transform(1, m) for m in range(4)]
    diff = e[1] - e[3]
    across = [pltpu.roll(diff[:, 128 * t : 128 * (t + 1)], 64, 1) for t in range(2)]
    turn = jnp.where(lax.broadcasted_iota(jnp.int32, (BLK, 128), 1) < 64, jnp.float32(-1.0), jnp.float32(1.0))
    diff = jnp.concatenate([turn * part_ for part_ in across], axis=1)
    sig[0] = (e[0] + e[2]) + (e[1] + e[3])
    sig[2] = (e[0] + e[2]) - (e[1] + e[3])
    sig[1] = (e[0] - e[2]) + diff
    sig[3] = (e[0] - e[2]) - diff

    def block(n):
        return lax.rem(x + 3 - n, 4)

    for n in range(4):
        for i in range(BLK // 16):
            rows = pl.ds(16 * i, 16)
            s0, s1 = sig[block(n), rows, 0:128], sig[block(n), rows, 128:256]
            group = (BLK // 16) * block(n) + i
            for d in range(16):
                v = s0 * gr[group, 2 * d] + s1 * gr[group, 2 * d + 1]
                pr[n % 2, 0, rows, pl.ds(128 * d, 128)], pr[n % 2, 1, rows, pl.ds(128 * d, 128)] = split(v)
        at = pl.ds(pl.multiple_of(BLK * block(n), 16), BLK)
        part[at, :] = (dot(pr[n % 2, 0], conv[...]) + dot(pr[n % 2, 1], conv[...])) + density
        for d in range(8 if n < 3 else 7):
            to = block(n) * 8 + lax.rem(2 * y + c + 4 + d if n < 3 else 2 * y + c + 1 + d, 8)
            pltpu.make_async_remote_copy(
                src_ref=part.at[pl.ds(NB * to, NB)], dst_ref=tsum.at[me], send_sem=send.at[2], recv_sem=recv.at[2],
                device_id={"ka": to}, device_id_type=MESH,
            ).start()
    pltpu.make_async_copy(part.at[pl.ds(NB * me, NB)], tsum.at[me], recv.at[2]).start()

    @pl.when(c == 1)
    def _():
        pl.semaphore_wait(barrier, HIST - 1)
        pl.semaphore_signal(go.at[1], inc=1, device_id={"ka": me - 1}, device_id_type=MESH)

    arrived(2, tsum)
    hbuf[z] = jnp.sum(tsum[...], axis=0)

    @pl.when(c == 0)
    def _():
        pl.semaphore_wait(go.at[1], 1)

    for d in (8, 7, 9, 6, 10, 5, 11, 4, 12, 3, 13, 2, 14, 1, 15):
        pltpu.make_async_remote_copy(
            src_ref=hbuf.at[z], dst_ref=hbuf.at[z], send_sem=send.at[3], recv_sem=recv.at[3],
            device_id={"hist": lax.rem(z + d, HIST)}, device_id_type=MESH,
        ).start()
    some = hbuf.at[pl.ds(0, HIST - 1)]
    pltpu.make_async_copy(some, some, recv.at[3]).wait()
    out[pl.ds(0, NB), :] = ham[...] + jnp.sum(hbuf[...], axis=0)
    out[pl.ds(NB, 24 - NB), :] = jnp.zeros((24 - NB, 128), jnp.float32)

    for n, ref in enumerate((rg, rw)):
        sent = ref.at[pl.ds(0, KA - 1)]
        pltpu.make_async_copy(sent, sent, send.at[n]).wait()
    sent = tsum.at[pl.ds(0, KA - 1)]
    pltpu.make_async_copy(sent, sent, send.at[2]).wait()
    pltpu.make_async_copy(some, some, send.at[3]).wait()


def propagate_kernel(eff_in, g, out, eff, gv, ov, coef, sem):
    nb = g.shape[0]
    groups = 3
    per = nb // groups
    fetch = [pltpu.make_async_copy(g.at[pl.ds(per * i, per)], gv.at[pl.ds(per * i, per)], sem.at[i]) for i in range(groups)]
    first = pltpu.make_async_copy(eff_in, eff, sem.at[2 * groups])
    first.start()
    for copy in fetch:
        copy.start()
    first.wait()

    e = eff[...] * jnp.float32(TIME_STEP)
    lane = lax.broadcasted_iota(jnp.int32, e.shape, 1)
    second = lane // 64
    for p in range(2):
        for b in range(8):
            from_imag = second == p
            index = jnp.where(from_imag, 64, 0) + (lane // 8) % 8 * 8 + b
            v = jnp.take_along_axis(e, index, axis=1)
            coef[8 * p + b] = jnp.where(from_imag | (second == 0), v, -v)

    lane8 = lax.broadcasted_iota(jnp.int32, (8, 128), 1)
    keep = lane8 % 8 == lax.broadcasted_iota(jnp.int32, (8, 128), 0)
    flush = []
    for i in range(groups):
        fetch[i].wait()
        for k in range(per * i, per * (i + 1)):
            rows = [
                jnp.where(keep, jnp.broadcast_to(coef[pb, pl.ds(k, 1), :], (8, 128)), jnp.float32(0.0)) for pb in range(16)
            ]
            mh, ml = split(jnp.concatenate(rows, axis=0))
            v = gv[k]
            vh, vl = split(v)
            ov[k] = v + dot3(vh, vl, mh, ml)
        copy = pltpu.make_async_copy(ov.at[pl.ds(per * i, per)], out.at[pl.ds(per * i, per)], sem.at[groups + i])
        copy.start()
        flush.append(copy)
    for copy in flush:
        copy.wait()


def per_device(green_row, screened, hamilton, equal_time, quad_class, live_count):
    nb, tb = NB, green_row.shape[0]
    g3 = green_row.transpose(1, 0, 2)
    w3 = screened.transpose(1, 0, 2)
    f32, bf16 = jnp.float32, jnp.bfloat16
    vmem, hbm = (pl.BlockSpec(memory_space=s) for s in (pltpu.VMEM, pltpu.HBM))
    eff = pl.pallas_call(
        collide_kernel,
        out_shape=jax.ShapeDtypeStruct((24, 128), f32),
        in_specs=[hbm] * 8,
        out_specs=vmem,
        scratch_shapes=[
            pltpu.VMEM((nb, 128), f32),
            pltpu.VMEM((nb, 128), f32),
            pltpu.SMEM((tb,), jnp.int32),
            pltpu.SMEM((1, 1), jnp.int32),
            pltpu.VMEM((KA, nb, 2, 128), f32),
            pltpu.VMEM((KA, nb, 2, 128), f32),
            pltpu.VMEM((2, 4, SIDE, 2 * BLK), f32),
            pltpu.VMEM((2048, 128), bf16),
            pltpu.VMEM((2, NK, 2 * BLK), bf16),
            pltpu.VMEM((2, NK, 2 * BLK), bf16),
            pltpu.VMEM((4, 2 * BLK, 256), bf16),
            pltpu.VMEM((4, 2 * BLK, 256), bf16),
            pltpu.VMEM((2, NK, 256), f32),
            pltpu.VMEM((4, BLK, 256), f32),
            pltpu.VMEM((NK // 16, 32, 16, 128), f32),
            pltpu.VMEM((2, 2, BLK, 2048), bf16),
            pltpu.VMEM((NK, 128), f32),
            pltpu.VMEM((KA, nb, 128), f32),
            pltpu.VMEM((HIST, nb, 128), f32),
            pltpu.SemaphoreType.DMA((4,)),
            pltpu.SemaphoreType.DMA((4,)),
            pltpu.SemaphoreType.DMA((6,)),
            pltpu.SemaphoreType.REGULAR((2,)),
        ],
        compiler_params=pltpu.CompilerParams(collective_id=0, has_side_effects=True, vmem_limit_bytes=60 << 20),
        name="collide",
    )(
        g3.reshape(nb, KA, 2, 128), w3.reshape(nb, KA, 2, 128), hamilton, equal_time, quad_class, live_count.reshape(1, 1),
        jnp.asarray(phase_tables()), jnp.asarray(contract_table(), dtype=bf16),
    )
    stepped = pl.pallas_call(
        propagate_kernel,
        out_shape=jax.ShapeDtypeStruct((nb, tb, 128), f32),
        in_specs=[hbm, hbm],
        out_specs=hbm,
        scratch_shapes=[
            pltpu.VMEM((24, 128), f32),
            pltpu.VMEM((nb, tb, 128), f32),
            pltpu.VMEM((nb, tb, 128), f32),
            pltpu.VMEM((16, 24, 128), f32),
            pltpu.SemaphoreType.DMA((7,)),
        ],
        name="propagate",
    )(eff, g3)
    return stepped.transpose(1, 0, 2)


def solution(mesh):
    in_specs = (
        P("hist", "ka", None), P("hist", "ka", None), P("ka", None), P("ka", None), P("hist"), P("hist"),
    )
    return jax.shard_map(
        per_device, mesh=mesh, in_specs=in_specs, out_specs=P("hist", "ka", None), check_vma=False
    )
```

```python
import functools
import math

import jax
import jax.numpy as jnp
import numpy as np
from jax import lax
from jax.experimental import pallas as pl
from jax.experimental.pallas import tpu as pltpu
from jax.sharding import PartitionSpec as P

SIDE = 24
NK = SIDE * SIDE
TIME_STEP = 0.1
HUBBARD = 1.0
QUADRATURE = (0.375, 1.1666666, 0.9583333, 1.0)
MESH = pl.DeviceIdType.MESH
KA, HIST = 32, 16
NB = NK // KA
BLK = NK // 4

OFFSETS = sorted(
    ((dx, dy, dc) for dx in range(4) for dy in range(4) for dc in range(2) if dx or dy or dc),
    key=lambda p: -(min(p[0], 4 - p[0]) + min(p[1], 4 - p[1])),
)


def phase_tables():
    col = np.arange(BLK)
    major, minor = col // SIDE, col % SIDE
    out = np.zeros((2, 4, SIDE, 2 * BLK), np.float64)
    for i in range(SIDE):
        m, part = i // 6, i % 6
        for way, turn in ((0, (4 * part + m) * major), (1, part * (4 * major + m))):
            t1 = 2 * math.pi * (turn % SIDE) / SIDE
            t2 = 2 * math.pi * ((i * minor) % SIDE) / SIDE
            c1, s1, c2, s2 = np.cos(t1), np.sin(t1), np.cos(t2), np.sin(t2)
            out[way, 0, i] = np.concatenate([c1, s1]) / SIDE
            out[way, 1, i] = np.concatenate([s1, -c1]) / SIDE
            out[way, 2, i] = np.concatenate([c2, c2])
            out[way, 3, i] = np.concatenate([s2, s2])
    return out.astype(np.float32)


def contract_table():
    out = np.zeros((16 * 128, 128), np.float32)
    for d in range(16):
        for i in range(128):
            p, a = i // 64, (i // 8) % 8
            block = (i // 8 + d) % 16
            q, c = block // 8, block % 8
            if p == q:
                out[d * 128 + i, 8 * a + c] = -1.0
            else:
                out[d * 128 + i, 64 + 8 * a + c] = 1.0 if p == 0 else -1.0
    return out


def split(v):
    high = v.astype(jnp.bfloat16)
    return high, (v - high.astype(jnp.float32)).astype(jnp.bfloat16)


def dot(a, b):
    return jnp.dot(a, b, preferred_element_type=jnp.float32)


def dot3(ah, al, bh, bl):
    return dot(ah, bh) + (dot(al, bh) + dot(ah, bl))


def collide_kernel(
    g, w, ham_in, eq_in, qc_in, lc_in, tab, con, out,
    ham, eq, qc, lc, rg, rw, tabv, conv, mh, ml, yh, yl, lat, sig, gr, pr, part, tsum, hbuf,
    send, recv, lsem, go,
):
    me = lax.axis_index("ka")
    z = lax.axis_index("hist")
    x, y, c = me // 8, (me // 2) % 4, me % 2

    def peer(dx, dy, dc):
        return (lax.rem(x + dx, 4) * 4 + lax.rem(y + dy, 4)) * 2 + lax.rem(c + dc, 2)

    tab_copy = pltpu.make_async_copy(tab, tabv, lsem.at[0])
    con_copy = pltpu.make_async_copy(con, conv, lsem.at[1])
    small = [
        pltpu.make_async_copy(a, b, lsem.at[2 + i]) for i, (a, b) in enumerate(((qc_in, qc), (lc_in, lc), (ham_in, ham), (eq_in, eq)))
    ]
    barrier = pltpu.get_barrier_semaphore()
    chip = me // 2
    for d in range(1, 16):
        pl.semaphore_signal(barrier, inc=1, device_id={"ka": 2 * lax.rem(chip + d, 16)}, device_id_type=MESH)

    @pl.when(c == 1)
    def _():
        pl.semaphore_signal(barrier, inc=1, device_id={"ka": me - 1}, device_id_type=MESH)

    tab_copy.start()
    con_copy.start()
    for copy in small:
        copy.start()

    @pl.when(c == 0)
    def _():
        pl.semaphore_wait(barrier, KA - 1)
        pl.semaphore_signal(go.at[0], inc=1, device_id={"ka": me + 1}, device_id_type=MESH)

    @pl.when(c == 1)
    def _():
        pl.semaphore_wait(go.at[0], 1)

    for n, (src, dst) in enumerate(((g, rg), (w, rw))):
        for d in OFFSETS:
            to = peer(*d)
            pltpu.make_async_remote_copy(
                src_ref=src.at[:, to], dst_ref=dst.at[me], send_sem=send.at[n], recv_sem=recv.at[n],
                device_id={"ka": to}, device_id_type=MESH,
            ).start()
        pltpu.make_async_copy(src.at[:, me], dst.at[me], recv.at[n]).start()

    @pl.when(c == 1)
    def _():
        for d in range(1, HIST):
            pl.semaphore_signal(barrier, inc=1, device_id={"hist": lax.rem(z + d, HIST)}, device_id_type=MESH)

    def arrived(n, dst):
        pltpu.make_async_copy(dst, dst, recv.at[n]).wait()

    lane = lax.broadcasted_iota(jnp.int32, (8, 128), 1)
    sign = jnp.where(lane < 64, jnp.float32(1.0), jnp.float32(-1.0))

    tab_copy.wait()

    def build(i, _):
        for way in range(2):
            rows = []
            for h in range(2):
                part = pl.ds(2 * i + h, 1)
                rows.append(tabv[way, 0, part, :] * tabv[way, 2] - tabv[way, 1, part, :] * tabv[way, 3])
            high, low = split(jnp.concatenate(rows, axis=0))
            at = pl.ds(pl.multiple_of(48 * i, 16), 48)
            mh[way, at, :] = high
            ml[way, at, :] = low
        return 0

    lax.fori_loop(0, SIDE // 2, build, 0)

    for copy in small:
        copy.wait()

    def weight(t):
        s = 2 * me + t
        q = qc[s]
        value = jnp.float32(0.0)
        for i in range(4):
            value = jnp.where(q == i, jnp.float32(np.float32(TIME_STEP) * np.float32(QUADRATURE[i])), value)
        return jnp.where(s < lc[0, 0], value, jnp.float32(0.0))

    weights = (weight(0), weight(1))
    sign16 = jnp.concatenate([sign, sign], axis=0)
    rg2, rw2 = rg.reshape(2 * NK, 128), rw.reshape(2 * NK, 128)

    arrived(0, rg)

    def put(m, row, t, v, turned):
        col = pl.ds(128 * t, 128)
        yh[m, pl.ds(row, 16), col], yl[m, pl.ds(row, 16), col] = split(v)
        yh[m, pl.ds(row + BLK, 16), col], yl[m, pl.ds(row + BLK, 16), col] = split(turned)

    def stage(i, _):
        row = pl.multiple_of(16 * i, 16)
        for t in range(2):
            v = [rg2[pl.ds(2 * (row + BLK * j) + t, 16, stride=2), :] for j in range(4)]
            w_ = [pltpu.roll(e, 64, 1) * sign16 for e in v]
            even, odd, even_, odd_ = v[0] + v[2], v[1] + v[3], w_[0] + w_[2], w_[1] + w_[3]
            put(0, row, t, even + odd, even_ + odd_)
            put(2, row, t, even - odd, even_ - odd_)
            even, odd, even_, odd_ = v[0] - v[2], v[1] - v[3], w_[0] - w_[2], w_[1] - w_[3]
            put(1, row, t, even + odd_, even_ - odd)
            put(3, row, t, even - odd_, even_ + odd)
        return 0

    lax.fori_loop(0, BLK // 16, stage, 0)

    def transform(way, m):
        at = pl.ds(BLK * m, BLK)
        return dot3(mh[way, at, :], ml[way, at, :], yh[m], yl[m])

    for m in range(4):
        v = transform(0, m)
        at = pl.ds(BLK * m, BLK)
        lat[0, at, :] = v
        for t in range(2):
            lat[1, at, pl.ds(128 * t, 128)] = pltpu.roll(v[:, 128 * t : 128 * (t + 1)], 64, 1)

    def rolled(i, _):
        for u in range(2):
            row = pl.multiple_of(32 * i + 16 * u, 16)
            for t in range(2):
                v = rg2[pl.ds(2 * row + t, 16, stride=2), :] * weights[t]
                for d in range(16):
                    gr[2 * i + u, 2 * d + t] = pltpu.roll(v, 128 - 8 * d, 1) if d else v
        return 0

    lax.fori_loop(0, NK // 32, rolled, 0)
    con_copy.wait()
    diag = (lax.broadcasted_iota(jnp.int32, (NB, 128), 1) - 64) % 9 == 0
    diag = diag & (lax.broadcasted_iota(jnp.int32, (NB, 128), 1) >= 64)
    occupied = jnp.sum(jnp.where(diag, eq[...], jnp.float32(0.0)))
    lane1 = lax.broadcasted_iota(jnp.int32, (1, 128), 1)
    density = jnp.where((lane1 % 9 == 0) & (lane1 < 64), occupied * jnp.float32(HUBBARD / NK / HIST), jnp.float32(0.0))

    arrived(1, rw)

    real = sign16 > 0

    def product(i, _):
        for pair in range(3):
            m = i
            for u in range(3):
                row = pl.multiple_of(48 * pair + 16 * u, 16)
                at = pl.ds(pl.multiple_of(BLK * m + 48 * pair + 16 * u, 16), 16)
                for t in range(2):
                    col = pl.ds(128 * t, 128)
                    halves = []
                    for h in range(2):
                        e = 2 * u + h
                        start = ((8 * pair + 4 * (e // 3) + m) * SIDE + 8 * (e % 3)) * 2 + t
                        halves.append(rw2[pl.ds(start, 8, stride=2), :])
                    v = jnp.concatenate(halves, axis=0)
                    same, cross = lat[0, at, col] * v, lat[1, at, col] * v
                    own = -jnp.where(real, cross, same)
                    other = jnp.where(real, same, -cross)
                    put(m, row, t, own + pltpu.roll(other, 64, 1), -sign16 * (pltpu.roll(own, 64, 1) + other))
        return 0

    lax.fori_loop(0, 4, product, 0)

    e = [transform(1, m) for m in range(4)]
    diff = e[1] - e[3]
    across = [pltpu.roll(diff[:, 128 * t : 128 * (t + 1)], 64, 1) for t in range(2)]
    turn = jnp.where(lax.broadcasted_iota(jnp.int32, (BLK, 128), 1) < 64, jnp.float32(-1.0), jnp.float32(1.0))
    diff = jnp.concatenate([turn * part_ for part_ in across], axis=1)
    sig[0] = (e[0] + e[2]) + (e[1] + e[3])
    sig[2] = (e[0] + e[2]) - (e[1] + e[3])
    sig[1] = (e[0] - e[2]) + diff
    sig[3] = (e[0] - e[2]) - diff

    def block(n):
        return lax.rem(x + 3 - n, 4)

    for n in range(4):
        for i in range(BLK // 16):
            rows = pl.ds(16 * i, 16)
            s0, s1 = sig[block(n), rows, 0:128], sig[block(n), rows, 128:256]
            group = (BLK // 16) * block(n) + i
            for d in range(16):
                v = s0 * gr[group, 2 * d] + s1 * gr[group, 2 * d + 1]
                pr[n % 2, 0, rows, pl.ds(128 * d, 128)], pr[n % 2, 1, rows, pl.ds(128 * d, 128)] = split(v)
        at = pl.ds(pl.multiple_of(BLK * block(n), 16), BLK)
        both = dot(pr[n % 2].reshape(2 * BLK, 2048), conv[...])
        part[at, :] = (both[:BLK] + both[BLK:]) + density
        for d in range(8 if n < 3 else 7):
            to = block(n) * 8 + lax.rem(2 * y + c + 4 + d if n < 3 else 2 * y + c + 1 + d, 8)
            pltpu.make_async_remote_copy(
                src_ref=part.at[pl.ds(NB * to, NB)], dst_ref=tsum.at[me], send_sem=send.at[2], recv_sem=recv.at[2],
                device_id={"ka": to}, device_id_type=MESH,
            ).start()
    pltpu.make_async_copy(part.at[pl.ds(NB * me, NB)], tsum.at[me], recv.at[2]).start()

    @pl.when(c == 1)
    def _():
        pl.semaphore_wait(barrier, HIST - 1)
        pl.semaphore_signal(go.at[1], inc=1, device_id={"ka": me - 1}, device_id_type=MESH)

    arrived(2, tsum)
    hbuf[z] = jnp.sum(tsum[...], axis=0)

    @pl.when(c == 0)
    def _():
        pl.semaphore_wait(go.at[1], 1)

    for d in (8, 7, 9, 6, 10, 5, 11, 4, 12, 3, 13, 2, 14, 1, 15):
        pltpu.make_async_remote_copy(
            src_ref=hbuf.at[z], dst_ref=hbuf.at[z], send_sem=send.at[3], recv_sem=recv.at[3],
            device_id={"hist": lax.rem(z + d, HIST)}, device_id_type=MESH,
        ).start()
    some = hbuf.at[pl.ds(0, HIST - 1)]
    pltpu.make_async_copy(some, some, recv.at[3]).wait()
    out[pl.ds(0, NB), :] = ham[...] + jnp.sum(hbuf[...], axis=0)
    out[pl.ds(NB, 24 - NB), :] = jnp.zeros((24 - NB, 128), jnp.float32)

    for n, ref in enumerate((rg, rw)):
        sent = ref.at[pl.ds(0, KA - 1)]
        pltpu.make_async_copy(sent, sent, send.at[n]).wait()
    sent = tsum.at[pl.ds(0, KA - 1)]
    pltpu.make_async_copy(sent, sent, send.at[2]).wait()
    pltpu.make_async_copy(some, some, send.at[3]).wait()


def propagate_kernel(eff_in, g, out, eff, gv, ov, coef, sem):
    nb = g.shape[0]
    groups = 3
    per = nb // groups
    fetch = [pltpu.make_async_copy(g.at[pl.ds(per * i, per)], gv.at[pl.ds(per * i, per)], sem.at[i]) for i in range(groups)]
    first = pltpu.make_async_copy(eff_in, eff, sem.at[2 * groups])
    first.start()
    for copy in fetch:
        copy.start()
    first.wait()

    e = eff[...] * jnp.float32(TIME_STEP)
    lane = lax.broadcasted_iota(jnp.int32, e.shape, 1)
    second = lane // 64
    for p in range(2):
        for b in range(8):
            from_imag = second == p
            index = jnp.where(from_imag, 64, 0) + (lane // 8) % 8 * 8 + b
            v = jnp.take_along_axis(e, index, axis=1)
            coef[8 * p + b] = jnp.where(from_imag | (second == 0), v, -v)

    lane8 = lax.broadcasted_iota(jnp.int32, (8, 128), 1)
    keep = lane8 % 8 == lax.broadcasted_iota(jnp.int32, (8, 128), 0)
    flush = []
    for i in range(groups):
        fetch[i].wait()
        for k in range(per * i, per * (i + 1)):
            rows = [
                jnp.where(keep, jnp.broadcast_to(coef[pb, pl.ds(k, 1), :], (8, 128)), jnp.float32(0.0)) for pb in range(16)
            ]
            mh, ml = split(jnp.concatenate(rows, axis=0))
            v = gv[k]
            vh, vl = split(v)
            both = dot(vh, jnp.concatenate([mh, ml], axis=1))
            ov[k] = v + (both[:, :128] + (both[:, 128:] + dot(vl, mh)))
        copy = pltpu.make_async_copy(ov.at[pl.ds(per * i, per)], out.at[pl.ds(per * i, per)], sem.at[groups + i])
        copy.start()
        flush.append(copy)
    for copy in flush:
        copy.wait()


def per_device(green_row, screened, hamilton, equal_time, quad_class, live_count):
    nb, tb = NB, green_row.shape[0]
    g3 = green_row.transpose(1, 0, 2)
    w3 = screened.transpose(1, 0, 2)
    f32, bf16 = jnp.float32, jnp.bfloat16
    vmem, hbm = (pl.BlockSpec(memory_space=s) for s in (pltpu.VMEM, pltpu.HBM))
    eff = pl.pallas_call(
        collide_kernel,
        out_shape=jax.ShapeDtypeStruct((24, 128), f32),
        in_specs=[hbm] * 8,
        out_specs=vmem,
        scratch_shapes=[
            pltpu.VMEM((nb, 128), f32),
            pltpu.VMEM((nb, 128), f32),
            pltpu.SMEM((tb,), jnp.int32),
            pltpu.SMEM((1, 1), jnp.int32),
            pltpu.VMEM((KA, nb, 2, 128), f32),
            pltpu.VMEM((KA, nb, 2, 128), f32),
            pltpu.VMEM((2, 4, SIDE, 2 * BLK), f32),
            pltpu.VMEM((2048, 128), bf16),
            pltpu.VMEM((2, NK, 2 * BLK), bf16),
            pltpu.VMEM((2, NK, 2 * BLK), bf16),
            pltpu.VMEM((4, 2 * BLK, 256), bf16),
            pltpu.VMEM((4, 2 * BLK, 256), bf16),
            pltpu.VMEM((2, NK, 256), f32),
            pltpu.VMEM((4, BLK, 256), f32),
            pltpu.VMEM((NK // 16, 32, 16, 128), f32),
            pltpu.VMEM((2, 2, BLK, 2048), bf16),
            pltpu.VMEM((NK, 128), f32),
            pltpu.VMEM((KA, nb, 128), f32),
            pltpu.VMEM((HIST, nb, 128), f32),
            pltpu.SemaphoreType.DMA((4,)),
            pltpu.SemaphoreType.DMA((4,)),
            pltpu.SemaphoreType.DMA((6,)),
            pltpu.SemaphoreType.REGULAR((2,)),
        ],
        compiler_params=pltpu.CompilerParams(collective_id=0, has_side_effects=True, vmem_limit_bytes=60 << 20),
        name="collide",
    )(
        g3.reshape(nb, KA, 2, 128), w3.reshape(nb, KA, 2, 128), hamilton, equal_time, quad_class, live_count.reshape(1, 1),
        jnp.asarray(phase_tables()), jnp.asarray(contract_table(), dtype=bf16),
    )
    stepped = pl.pallas_call(
        propagate_kernel,
        out_shape=jax.ShapeDtypeStruct((nb, tb, 128), f32),
        in_specs=[hbm, hbm],
        out_specs=hbm,
        scratch_shapes=[
            pltpu.VMEM((24, 128), f32),
            pltpu.VMEM((nb, tb, 128), f32),
            pltpu.VMEM((nb, tb, 128), f32),
            pltpu.VMEM((16, 24, 128), f32),
            pltpu.SemaphoreType.DMA((7,)),
        ],
        name="propagate",
    )(eff, g3)
    return stepped.transpose(1, 0, 2)


def solution(mesh):
    in_specs = (
        P("hist", "ka", None), P("hist", "ka", None), P("ka", None), P("ka", None), P("hist"), P("hist"),
    )
    return jax.shard_map(
        per_device, mesh=mesh, in_specs=in_specs, out_specs=P("hist", "ka", None), check_vma=False
    )
```
